1024 devices in a mesh: chan: 64 (over z_lo, x, core), tile: 16 (over y, z_hi).
Axes of the slice: x: 8, y: 8, z: 8 (z_hi: 2, z_lo: 4; z = z_hi * 4 + z_lo), core: 2. Of those that a mesh axis runs over, the one named last changes fastest.
Arguments:
- voltages: bfloat16 [16, 128, 555008], P('tile', 'chan'), may hold values from -6 to 6
- fir_taps: float32 [16, 2048], replicated, may hold values from -4 to 4
- channels: int32 [64], replicated, may hold values from 0 to 2047
- input_good_mask: int32 [16, 128], P('tile', 'chan'), may hold values 0 or 1
- tile_map: int32 [64, 16], replicated, may hold values from 0 to 15, each once within a row
Outputs:
- visibilities: bfloat16 [64, 16, 2, 512, 512], P('chan', 'tile')
The draws below stay inside these ranges and needn't reach their ends.
Inputs may be any that keep to these rules, and one draw needn't show every extreme that they name: `tile_map`: for every channel, every tile of the 4 x 4 grid, numbered row by row, stands in exactly one slot.
All inputs are finite; a program needn't handle non-finite values. No bound on the sum of `input_good_mask` on one device may be relied on, other than what follows from the above.
Results may differ from the reference program's by a relative error of at most 0.0077.
Values may be sent and summed in bfloat16 or wider, within the bound.
A program may use at most 32 MiB of HBM per device.

```python
import math
import jax
import jax.numpy as jnp
from jax import lax

TRANSFORM_LENGTH = 2048
FILTER_TAPS = 16
SPECTRA_SUMMED = 256
CHANS = 64
INPUTS = 2048
PIECE = 128
GRID = 4
TILE_SIDE = 512
SAMPLES = 555008
N_TILE = 16


def with_ends(entries, rng, least, top_value):
    longest = entries.shape.index(max(entries.shape))
    spots = []
    for shift in (0, 1):
        where = [jax.random.randint(jax.random.fold_in(rng, axis), (), 0, length) for axis, length in enumerate(entries.shape)]
        where[longest] = (where[longest] + shift) % entries.shape[longest]
        spots.append(tuple(where))
    return entries.at[spots[0]].set(least).at[spots[1]].set(top_value)


def level_of(key, shape, split, low, largest):
    gain, own = 1.0, jax.random.fold_in(key, 6)
    for dim, shards_of in split:
        steps = jnp.exp(jax.random.uniform(jax.random.fold_in(own, dim), (shards_of,), jnp.float32, low / len(split), largest / len(split)))
        gain = gain * jnp.repeat(steps, shape[dim] // shards_of).reshape([-1 if axis == dim else 1 for axis in range(len(shape))])
    return gain


def centred(key, extent, deviation, most, split=(), kind=jnp.bfloat16):
    result = deviation * jax.random.normal(key, extent, jnp.float32)
    if split:
        result = result * level_of(key, extent, split, -0.22, 0.18)
    return jnp.clip(result, -most, most).astype(kind)


def setup_inputs(seed: int = 0) -> dict:
    keys = jax.random.split(jax.random.key(seed), 6)
    return {
        "voltages": centred(keys[0], (N_TILE, PIECE, SAMPLES), 1.0, 6.0, ((0, 16), (1, 64))),
        "fir_taps": centred(keys[1], (FILTER_TAPS, TRANSFORM_LENGTH), 0.25, 4.0, (), jnp.float32),
        "channels": with_ends(jax.random.randint(keys[2], (CHANS,), 0, TRANSFORM_LENGTH), jax.random.fold_in(keys[2], 1), 0, TRANSFORM_LENGTH - 1).astype(jnp.int32),
        "input_good_mask": with_ends((jax.random.randint(keys[3], (N_TILE, PIECE), 0, 8) < 7).astype(jnp.int32), jax.random.fold_in(keys[3], 1), 0, 1),
        "tile_map": jax.vmap(lambda own: jax.random.permutation(own, N_TILE))(jax.random.split(keys[4], CHANS)).reshape((CHANS, N_TILE)).astype(jnp.int32),
    }


def dft_rows(channels):
    sample = jnp.arange(TRANSFORM_LENGTH, dtype=jnp.int32)
    phase = channels[:, None].astype(jnp.int32) * sample[None, :] % TRANSFORM_LENGTH
    angle = phase.astype(jnp.float32) * (2.0 * math.pi / TRANSFORM_LENGTH)
    factor = 1.0 / math.sqrt(TRANSFORM_LENGTH)
    return jnp.concatenate([jnp.cos(angle) * factor, -jnp.sin(angle) * factor], axis=0).astype(jnp.bfloat16)

def filtered_block(sample_block, fir_taps):
    running_total = jnp.zeros((sample_block.shape[0], SPECTRA_SUMMED, TRANSFORM_LENGTH), jnp.float32)
    for tap_index in range(FILTER_TAPS):
        running_total = running_total + fir_taps[tap_index][None, None, :] * sample_block[:, tap_index:tap_index + SPECTRA_SUMMED, :].astype(jnp.float32)
    return running_total.astype(jnp.bfloat16)

def reference(voltages, fir_taps, channels, input_good_mask, tile_map):
    dft_table = dft_rows(channels).astype(jnp.float32)
    blocks = voltages.reshape(N_TILE, PIECE, SPECTRA_SUMMED + FILTER_TAPS - 1, TRANSFORM_LENGTH)
    flag_rows = input_good_mask.astype(jnp.float32)

    def one_group(operands):
        sample_block, flag_row = operands
        filtered = filtered_block(sample_block, fir_taps).astype(jnp.float32)
        spectra = jnp.einsum('kn,bsn->kbs', dft_table, filtered)
        return (spectra * flag_row[None, :, None]).astype(jnp.bfloat16)
    groups = lax.map(one_group, (blocks, flag_rows))
    spectra_all = jnp.transpose(groups, (1, 0, 2, 3)).reshape(2, CHANS, INPUTS, SPECTRA_SUMMED)
    per_channel = jnp.transpose(spectra_all, (1, 0, 2, 3))

    def one_channel(operands):
        chan_data, slot_tiles = operands
        chan_data = chan_data.astype(jnp.float32)

        def one_slot(slot):
            tile = slot_tiles[slot]
            row_start = (tile // GRID * TILE_SIDE).astype(jnp.int32)
            col_start = (tile % GRID * TILE_SIDE).astype(jnp.int32)
            rows = lax.dynamic_slice_in_dim(chan_data, row_start, TILE_SIDE, 1)
            cols = lax.dynamic_slice_in_dim(chan_data, col_start, TILE_SIDE, 1)
            swapped = jnp.stack([cols[1], -cols[0]], axis=0)
            real_part = jnp.einsum('xis,xjs->ij', rows, cols)
            imag_part = jnp.einsum('xis,xjs->ij', rows, swapped)
            return (jnp.stack([real_part, imag_part], axis=0) * (1.0 / SPECTRA_SUMMED)).astype(jnp.bfloat16)
        return lax.map(one_slot, jnp.arange(N_TILE, dtype=jnp.int32))
    return lax.map(one_channel, (per_channel, tile_map))
```

```python
import math

import jax
import jax.numpy as jnp
from jax import lax
from jax.experimental import pallas as pl
from jax.experimental.pallas import tpu as pltpu
from jax.sharding import PartitionSpec as P

TRANSFORM_LENGTH = 2048
FILTER_TAPS = 16
SPECTRA_SUMMED = 256
MESH = pl.DeviceIdType.MESH


def dft_rows(channels):
    sample = jnp.arange(TRANSFORM_LENGTH, dtype=jnp.int32)
    phase = channels[:, None] * sample[None, :] % TRANSFORM_LENGTH
    angle = phase.astype(jnp.float32) * (2.0 * math.pi / TRANSFORM_LENGTH)
    factor = 1.0 / math.sqrt(TRANSFORM_LENGTH)
    return jnp.concatenate([jnp.cos(angle) * factor, -jnp.sin(angle) * factor], axis=0).astype(
        jnp.bfloat16
    )


def correlate_kernel(
    n_chan, n_tile, map_ref, send_ref, out_ref, turned, whole,
    turn_send, turn_recv, ring_send, ring_recv, pair_send, pair_recv,
):
    me = lax.axis_index("chan")
    here = lax.axis_index("tile")
    ahead, behind = lax.rem(here + 2, n_tile), lax.rem(here + n_tile - 2, n_tile)
    pair = here + 1 - 2 * lax.rem(here, 2)
    block_rows, width = whole.shape[1], whole.shape[2]
    grid_side = n_tile // 8 + 2
    side = block_rows * n_tile // grid_side

    barrier = pltpu.get_barrier_semaphore()

    def greet(step, _):
        peer = lax.rem(me + step, n_chan)
        pl.semaphore_signal(barrier, inc=1, device_id={"chan": peer}, device_id_type=MESH)
        return 0

    lax.fori_loop(1, n_chan, greet, 0)
    for other in (ahead, behind, pair):
        pl.semaphore_signal(barrier, inc=1, device_id={"tile": other}, device_id_type=MESH)
    pl.semaphore_wait(barrier, n_chan - 1 + 3)

    def turn(step, _):
        peer = lax.rem(me + step, n_chan)
        pltpu.make_async_remote_copy(
            src_ref=send_ref.at[peer], dst_ref=turned.at[me], send_sem=turn_send,
            recv_sem=turn_recv, device_id={"chan": peer}, device_id_type=MESH,
        ).start()
        return 0

    lax.fori_loop(1, n_chan, turn, 0)
    turned[me] = send_ref[me]
    pltpu.make_async_remote_copy(
        src_ref=send_ref.at[pl.ds(0, n_chan - 1)], dst_ref=turned.at[pl.ds(0, n_chan - 1)],
        send_sem=turn_send, recv_sem=turn_recv, device_id={"chan": me}, device_id_type=MESH,
    ).wait()
    whole[here] = turned[...].reshape(block_rows, width)

    def hop(direction, column, step):
        base = here if column == 0 else pair
        back = -2 * (step - 1) if direction == 0 else 2 * (step - 1)
        block = lax.rem(base + n_tile + back, n_tile)
        piece = whole.at[block]
        if step == n_tile // 4:
            half = block_rows // 2
            piece = whole.at[block, pl.ds(direction * half, half)]
        index = (direction, column, step - 1)
        return pltpu.make_async_remote_copy(
            src_ref=piece, dst_ref=piece, send_sem=ring_send.at[index],
            recv_sem=ring_recv.at[index],
            device_id={"tile": ahead if direction == 0 else behind}, device_id_type=MESH,
        )

    across = pltpu.make_async_remote_copy(
        src_ref=whole.at[here], dst_ref=whole.at[here], send_sem=pair_send, recv_sem=pair_recv,
        device_id={"tile": pair}, device_id_type=MESH,
    )
    across.start()
    last = n_tile // 4
    order = [(0, 1), (0, 2), (1, 1), (0, 3), (1, 2), (0, 4), (1, 3), (1, 4)]
    for column, step in order:
        if step == 1 and column == 1:
            across.wait_recv()
        for direction in (0, 1):
            if step > 1:
                hop(direction, column, step - 1).wait_recv()
            hop(direction, column, step).start()
    for column in (0, 1):
        for direction in (0, 1):
            hop(direction, column, last).wait_recv()
    across.wait_send()
    for column, step in order:
        for direction in (0, 1):
            hop(direction, column, step).wait_send()

    tile = map_ref[me, here]
    per_side = n_tile // grid_side
    rows = whole[pl.ds(lax.div(tile, grid_side) * per_side, per_side)].reshape(side, width)
    cols = whole[pl.ds(lax.rem(tile, grid_side) * per_side, per_side)].reshape(side, width)
    half = width // 2
    swapped = jnp.concatenate([cols[:, half:], -cols[:, :half]], axis=1)
    contract = (((1,), (1,)), ((), ()))
    scale = 1.0 / SPECTRA_SUMMED
    real_part = lax.dot_general(rows, cols, contract, preferred_element_type=jnp.float32)
    out_ref[0, 0, 0] = (real_part * scale).astype(out_ref.dtype)
    imag_part = lax.dot_general(rows, swapped, contract, preferred_element_type=jnp.float32)
    out_ref[0, 0, 1] = (imag_part * scale).astype(out_ref.dtype)


def on_device(voltages, fir_taps, channels, input_good_mask, tile_map):
    antennas = voltages.shape[1]
    sample_block = voltages.reshape(antennas, SPECTRA_SUMMED + FILTER_TAPS - 1, TRANSFORM_LENGTH)
    running_total = jnp.zeros((antennas, SPECTRA_SUMMED, TRANSFORM_LENGTH), jnp.float32)
    for tap_index in range(FILTER_TAPS):
        running_total = running_total + fir_taps[tap_index][None, None, :] * sample_block[
            :, tap_index : tap_index + SPECTRA_SUMMED, :
        ].astype(jnp.float32)
    filtered = running_total.astype(jnp.bfloat16)
    dft_table = dft_rows(channels)
    spectra = jnp.einsum("kn,asn->kas", dft_table, filtered, preferred_element_type=jnp.float32)
    flags = input_good_mask.reshape(1, antennas, 1).astype(jnp.float32)
    spectra = (spectra * flags).astype(jnp.bfloat16)
    n_channels = channels.shape[0]
    n_chan, n_tile = lax.axis_size("chan"), lax.axis_size("tile")
    spectra = spectra.reshape(2, n_channels, antennas, SPECTRA_SUMMED)
    send = jnp.transpose(spectra, (1, 2, 0, 3)).reshape(n_channels, antennas, 2 * SPECTRA_SUMMED)

    block_rows, width = antennas * n_chan, 2 * SPECTRA_SUMMED
    side = block_rows * n_tile // (n_tile // 8 + 2)
    vmem = pl.BlockSpec(memory_space=pltpu.VMEM)
    hops = (2, 2, n_tile // 4)
    return pl.pallas_call(
        lambda *refs: correlate_kernel(n_chan, n_tile, *refs),
        name="correlate",
        out_shape=jax.ShapeDtypeStruct((1, 1, 2, side, side), jnp.bfloat16),
        in_specs=[pl.BlockSpec(memory_space=pltpu.SMEM), vmem],
        out_specs=vmem,
        scratch_shapes=[
            pltpu.VMEM((n_chan, antennas, width), jnp.bfloat16),
            pltpu.VMEM((n_tile, block_rows, width), jnp.bfloat16),
            pltpu.SemaphoreType.DMA,
            pltpu.SemaphoreType.DMA,
            pltpu.SemaphoreType.DMA(hops),
            pltpu.SemaphoreType.DMA(hops),
            pltpu.SemaphoreType.DMA,
            pltpu.SemaphoreType.DMA,
        ],
        compiler_params=pltpu.CompilerParams(
            collective_id=0, has_side_effects=True, vmem_limit_bytes=32 * 1024 * 1024
        ),
    )(tile_map, send)


def solution(mesh):
    in_specs = (P("tile", "chan", None), P(), P(), P("tile", "chan"), P())
    out_specs = P("chan", "tile", None, None, None)
    return jax.shard_map(
        on_device, mesh=mesh, in_specs=in_specs, out_specs=out_specs, check_vma=False
    )
```

```python
import math

import jax
import jax.numpy as jnp
from jax import lax
from jax.experimental import pallas as pl
from jax.experimental.pallas import tpu as pltpu
from jax.sharding import PartitionSpec as P

TRANSFORM_LENGTH = 2048
FILTER_TAPS = 16
SPECTRA_SUMMED = 256
MESH = pl.DeviceIdType.MESH

LANES = 128
GROUPS = TRANSFORM_LENGTH // LANES
FRAMES = SPECTRA_SUMMED + FILTER_TAPS - 1
CHUNK = LANES
CHUNKS = SPECTRA_SUMMED // CHUNK
BY_LANES = (((1,), (1,)), ((), ()))

RING_ORDER = (
    (0, 0, 1), (1, 0, 1), (0, 0, 2), (1, 0, 2), (0, 1, 1), (0, 0, 3), (1, 0, 3), (1, 1, 1),
    (0, 1, 2), (0, 0, 4), (1, 0, 4), (1, 1, 2), (0, 1, 3), (1, 1, 3), (0, 1, 4), (1, 1, 4),
)


def fill_table(channels_row, table):
    n = channels_row.shape[1]
    down = lax.broadcasted_iota(jnp.int32, (n, n), 0)
    along = lax.broadcasted_iota(jnp.int32, (n, n), 1)
    picked = jnp.where(down == along, channels_row.astype(jnp.float32), 0.0)
    lane = lax.broadcasted_iota(jnp.int32, (n, LANES), 1).astype(jnp.float32)
    phase = jnp.sum(picked, axis=1, keepdims=True) * lane
    low = phase - TRANSFORM_LENGTH * jnp.floor(phase * (1.0 / TRANSFORM_LENGTH))
    low = low * (2.0 * math.pi / TRANSFORM_LENGTH)
    high = phase - GROUPS * jnp.floor(phase * (1.0 / GROUPS))
    high = high * (2.0 * math.pi / GROUPS)
    factor = 1.0 / math.sqrt(TRANSFORM_LENGTH)
    cos_low, sin_low = jnp.cos(low) * factor, jnp.sin(low) * factor
    cos_high, sin_high = jnp.cos(high), jnp.sin(high)
    for group in range(GROUPS):
        lanes = pl.ds(group * LANES, LANES)
        cos_g, sin_g = cos_high[:, group : group + 1], sin_high[:, group : group + 1]
        table[pl.ds(0, n), lanes] = (cos_g * cos_low - sin_g * sin_low).astype(table.dtype)
        table[pl.ds(n, n), lanes] = (-(sin_g * cos_low + cos_g * sin_low)).astype(table.dtype)


def filter_group(group, chunk, slab, wide, taps, filtered):
    rows = 2 * (CHUNK + FILTER_TAPS)
    samples = slab.at[group].reshape(slab.shape[1] * 2, LANES)
    for row in range(0, rows, 16):
        wide[pl.ds(row, 16), :] = samples[pl.ds(2 * CHUNK * chunk + row, 16), :].astype(jnp.float32)
    lanes = pl.ds(group * LANES, LANES)
    weight = [jnp.broadcast_to(taps[pl.ds(j, 1), lanes], (8, LANES)) for j in range(FILTER_TAPS)]
    for antenna in (0, 1):
        for base in range(0, CHUNK, 64):
            total = [None] * 8
            for frame in range(64 + FILTER_TAPS - 8):
                window = wide[pl.ds(2 * (base + frame) + antenna, 8, stride=2), :]
                for part in range(8):
                    j = frame - 8 * part
                    if 0 <= j < FILTER_TAPS:
                        term = weight[j] * window
                        total[part] = term if total[part] is None else total[part] + term
            for part in range(0, 8, 2):
                pair = jnp.concatenate([total[part], total[part + 1]], axis=0)
                place = pl.ds(antenna * CHUNK + base + 8 * part, 16)
                filtered[place, lanes] = pair.astype(filtered.dtype)


def kernel(
    n_chan, n_tile, volts, taps_hbm, channels, flags, tile_map, out,
    slab, taps, wide, filtered, table, mixed, gathered, totals, *rest,
):
    send, whole = rest[:CHUNKS], rest[CHUNKS : 2 * CHUNKS]
    load_sem, taps_sem, turn_send, turn_recv, ring_send, ring_recv, pair_send, pair_recv = rest[
        2 * CHUNKS :
    ]
    me = lax.axis_index("chan")
    here = lax.axis_index("tile")
    ahead, behind = lax.rem(here + 2, n_tile), lax.rem(here + n_tile - 2, n_tile)
    pair = here + 1 - 2 * lax.rem(here, 2)
    last = n_tile // 4
    grid_side = n_tile // 8 + 2
    side = 2 * n_chan * n_tile // grid_side

    def load(group):
        return pltpu.make_async_copy(
            volts.at[:, group], slab.at[group, pl.ds(0, FRAMES)], load_sem.at[group]
        )

    load_taps = pltpu.make_async_copy(taps_hbm, taps, taps_sem)
    load_taps.start()
    for group in range(GROUPS):
        load(group).start()

    barrier = pltpu.get_barrier_semaphore()

    def greet(step, _):
        peer = lax.rem(me + step, n_chan)
        pl.semaphore_signal(barrier, inc=1, device_id={"chan": peer}, device_id_type=MESH)
        return 0

    lax.fori_loop(1, n_chan, greet, 0)
    for other in (ahead, behind, pair):
        pl.semaphore_signal(barrier, inc=1, device_id={"tile": other}, device_id_type=MESH)

    fill_table(channels[...], table)
    load_taps.wait()

    for chunk in range(CHUNKS):

        def filter_step(group, _):
            if chunk == 0:
                load(group).wait()
            filter_group(group, chunk, slab, wide, taps, filtered)
            return 0

        lax.fori_loop(0, GROUPS, filter_step, 0)
        spectra = lax.dot_general(
            table[...], filtered[...], BY_LANES, preferred_element_type=jnp.float32
        )
        for part in (0, 1):
            for antenna in (0, 1):
                flag = flags[0, antenna].astype(jnp.float32)
                block = spectra[
                    part * n_chan : (part + 1) * n_chan, antenna * CHUNK : (antenna + 1) * CHUNK
                ]
                mixed[pl.ds(antenna, n_chan, stride=2), :] = block * flag
            packed = send[chunk].at[part].reshape(2 * n_chan, LANES)
            packed[...] = mixed[...].astype(packed.dtype)
        if chunk == 0:
            pl.semaphore_wait(barrier, n_chan - 1 + 3)

        def turn(step, _):
            peer = lax.rem(me + step, n_chan)
            pltpu.make_async_remote_copy(
                src_ref=send[chunk].at[:, peer], dst_ref=whole[chunk].at[:, here, me],
                send_sem=turn_send.at[chunk], recv_sem=turn_recv.at[chunk],
                device_id={"chan": peer}, device_id_type=MESH,
            ).start()
            return 0

        lax.fori_loop(1, n_chan, turn, 0)
        whole[chunk][:, here, me] = send[chunk][:, me]

    def turned(chunk):
        return pltpu.make_async_remote_copy(
            src_ref=send[chunk].at[:, pl.ds(0, n_chan - 1)],
            dst_ref=whole[chunk].at[:, here, pl.ds(0, n_chan - 1)],
            send_sem=turn_send.at[chunk], recv_sem=turn_recv.at[chunk],
            device_id={"chan": me}, device_id_type=MESH,
        )

    def across(chunk):
        block = whole[chunk].at[:, here]
        return pltpu.make_async_remote_copy(
            src_ref=block, dst_ref=block, send_sem=pair_send.at[chunk],
            recv_sem=pair_recv.at[chunk], device_id={"tile": pair}, device_id_type=MESH,
        )

    def hop(chunk, direction, column, step):
        base = here if column == 0 else pair
        back = -2 * (step - 1) if direction == 0 else 2 * (step - 1)
        block = lax.rem(base + n_tile + back, n_tile)
        piece = whole[chunk].at[direction, block] if step == last else whole[chunk].at[:, block]
        index = (chunk, direction, column, step - 1)
        return pltpu.make_async_remote_copy(
            src_ref=piece, dst_ref=piece, send_sem=ring_send.at[index],
            recv_sem=ring_recv.at[index],
            device_id={"tile": ahead if direction == 0 else behind}, device_id_type=MESH,
        )

    for chunk, column, step in RING_ORDER:
        if step == 1 and column == 0:
            turned(chunk).wait()
            across(chunk).start()
        if step == 1 and column == 1:
            across(chunk).wait_recv()
        for direction in (0, 1):
            if step > 1:
                hop(chunk, direction, column, step - 1).wait_recv()
            hop(chunk, direction, column, step).start()

    tile = tile_map[here, me]
    for chunk in range(CHUNKS):
        for column in (0, 1):
            for direction in (0, 1):
                hop(chunk, direction, column, last).wait_recv()
        across(chunk).wait_send()
        for _, column, step in [entry for entry in RING_ORDER if entry[0] == chunk]:
            for direction in (0, 1):
                hop(chunk, direction, column, step).wait_send()
        inputs = 2 * n_chan * n_tile
        flat = whole[chunk].reshape(2 * inputs, LANES)
        for part in (0, 1):
            for block in range(grid_side):
                gathered[block, :, part * LANES : (part + 1) * LANES] = flat[
                    pl.ds(part * inputs + block * side, side), :
                ]
        rows = gathered[lax.div(tile, grid_side)]
        straight = gathered[lax.rem(tile, grid_side)]
        crossed = jnp.concatenate([straight[:, LANES:], -straight[:, :LANES]], axis=1)
        for part, cols in enumerate((straight, crossed)):
            product = lax.dot_general(rows, cols, BY_LANES, preferred_element_type=jnp.float32)
            if chunk > 0:
                product = product + totals[part]
            if chunk < CHUNKS - 1:
                totals[part] = product
            else:
                out[0, 0, part] = (product * (1.0 / SPECTRA_SUMMED)).astype(out.dtype)


def on_device(voltages, fir_taps, channels, input_good_mask, tile_map):
    n_chan, n_tile = lax.axis_size("chan"), lax.axis_size("tile")
    side = 2 * n_chan * n_tile // (n_tile // 8 + 2)
    volts = voltages.reshape(2, FRAMES, GROUPS, LANES).transpose(1, 2, 0, 3)
    vmem = pl.BlockSpec(memory_space=pltpu.VMEM)
    smem = pl.BlockSpec(memory_space=pltpu.SMEM)
    hbm = pl.BlockSpec(memory_space=pltpu.HBM)
    dma = pltpu.SemaphoreType.DMA
    hops = (CHUNKS, 2, 2, n_tile // 4)
    return pl.pallas_call(
        lambda *refs: kernel(n_chan, n_tile, *refs),
        name="channelize_correlate",
        out_shape=jax.ShapeDtypeStruct((1, 1, 2, side, side), jnp.bfloat16),
        in_specs=[hbm, hbm, vmem, smem, smem],
        out_specs=vmem,
        scratch_shapes=[
            pltpu.VMEM((GROUPS, FRAMES + 1, 2, LANES), jnp.bfloat16),
            pltpu.VMEM((FILTER_TAPS, TRANSFORM_LENGTH), jnp.float32),
            pltpu.VMEM((2 * (CHUNK + FILTER_TAPS), LANES), jnp.float32),
            pltpu.VMEM((2 * CHUNK, TRANSFORM_LENGTH), jnp.bfloat16),
            pltpu.VMEM((2 * n_chan, TRANSFORM_LENGTH), jnp.bfloat16),
            pltpu.VMEM((2 * n_chan, LANES), jnp.float32),
            pltpu.VMEM((n_tile // 8 + 2, side, 2 * LANES), jnp.bfloat16),
            pltpu.VMEM((2, side, side), jnp.float32),
            *[pltpu.VMEM((2, n_chan, 2, LANES), jnp.bfloat16)] * CHUNKS,
            *[pltpu.VMEM((2, n_tile, n_chan, 2, LANES), jnp.bfloat16)] * CHUNKS,
            dma((GROUPS,)),
            dma,
            dma((CHUNKS,)),
            dma((CHUNKS,)),
            dma(hops),
            dma(hops),
            dma((CHUNKS,)),
            dma((CHUNKS,)),
        ],
        compiler_params=pltpu.CompilerParams(
            collective_id=0, has_side_effects=True, vmem_limit_bytes=60 * 1024 * 1024
        ),
    )(volts, fir_taps, channels.reshape(1, -1), input_good_mask, tile_map.T)


def solution(mesh):
    in_specs = (P("tile", "chan", None), P(), P(), P("tile", "chan"), P())
    out_specs = P("chan", "tile", None, None, None)
    return jax.shard_map(
        on_device, mesh=mesh, in_specs=in_specs, out_specs=out_specs, check_vma=False
    )
```

```python
import math

import jax
import jax.numpy as jnp
from jax import lax
from jax.experimental import pallas as pl
from jax.experimental.pallas import tpu as pltpu
from jax.sharding import PartitionSpec as P

TRANSFORM_LENGTH = 2048
FILTER_TAPS = 16
SPECTRA_SUMMED = 256
MESH = pl.DeviceIdType.MESH

LANES = 128
GROUPS = TRANSFORM_LENGTH // LANES
FRAMES = SPECTRA_SUMMED + FILTER_TAPS - 1
CHUNK = LANES
CHUNKS = SPECTRA_SUMMED // CHUNK
BY_LANES = (((1,), (1,)), ((), ()))

RING_ORDER = (
    (0, 0, 1), (0, 0, 2), (0, 0, 3), (1, 0, 1), (0, 1, 1), (1, 0, 2), (0, 1, 2), (0, 0, 4),
    (1, 1, 1), (0, 1, 3), (1, 1, 2), (1, 0, 3), (1, 1, 3), (0, 1, 4), (1, 0, 4), (1, 1, 4),
)


def fill_table(channels_row, table):
    n = channels_row.shape[1]
    down = lax.broadcasted_iota(jnp.int32, (n, n), 0)
    along = lax.broadcasted_iota(jnp.int32, (n, n), 1)
    picked = jnp.where(down == along, channels_row.astype(jnp.float32), 0.0)
    lane = lax.broadcasted_iota(jnp.int32, (n, LANES), 1).astype(jnp.float32)
    phase = jnp.sum(picked, axis=1, keepdims=True) * lane
    low = phase - TRANSFORM_LENGTH * jnp.floor(phase * (1.0 / TRANSFORM_LENGTH))
    low = low * (2.0 * math.pi / TRANSFORM_LENGTH)
    high = phase - GROUPS * jnp.floor(phase * (1.0 / GROUPS))
    high = high * (2.0 * math.pi / GROUPS)
    factor = 1.0 / math.sqrt(TRANSFORM_LENGTH)
    cos_low, sin_low = jnp.cos(low) * factor, jnp.sin(low) * factor
    cos_high, sin_high = jnp.cos(high), jnp.sin(high)
    for group in range(GROUPS):
        lanes = pl.ds(group * LANES, LANES)
        cos_g, sin_g = cos_high[:, group : group + 1], sin_high[:, group : group + 1]
        table[pl.ds(0, n), lanes] = (cos_g * cos_low - sin_g * sin_low).astype(table.dtype)
        table[pl.ds(n, n), lanes] = (-(sin_g * cos_low + cos_g * sin_low)).astype(table.dtype)


def filter_group(group, chunk, slab, wide, taps, filtered):
    rows = 2 * (CHUNK + FILTER_TAPS)
    samples = slab.at[group].reshape(slab.shape[1] * 2, LANES)
    for row in range(0, rows, 16):
        wide[pl.ds(row, 16), :] = samples[pl.ds(2 * CHUNK * chunk + row, 16), :].astype(jnp.float32)
    lanes = pl.ds(group * LANES, LANES)
    weight = [jnp.broadcast_to(taps[pl.ds(j, 1), lanes], (8, LANES)) for j in range(FILTER_TAPS)]
    for antenna in (0, 1):
        for base in range(0, CHUNK, 64):
            total = [None] * 8
            for frame in range(64 + FILTER_TAPS - 8):
                window = wide[pl.ds(2 * (base + frame) + antenna, 8, stride=2), :]
                for part in range(8):
                    j = frame - 8 * part
                    if 0 <= j < FILTER_TAPS:
                        term = weight[j] * window
                        total[part] = term if total[part] is None else total[part] + term
            for part in range(0, 8, 2):
                pair = jnp.concatenate([total[part], total[part + 1]], axis=0)
                place = pl.ds(antenna * CHUNK + base + 8 * part, 16)
                filtered[place, lanes] = pair.astype(filtered.dtype)


def kernel(
    n_chan, n_tile, volts, taps_hbm, channels, flags, tile_map, out,
    slab, taps, wide, filtered, table, mixed, gathered, totals, *rest,
):
    send, whole = rest[:CHUNKS], rest[CHUNKS : 2 * CHUNKS]
    load_sem, taps_sem, turn_send, turn_recv, ring_send, ring_recv, pair_send, pair_recv = rest[
        2 * CHUNKS :
    ]
    me = lax.axis_index("chan")
    here = lax.axis_index("tile")
    ahead, behind = lax.rem(here + 2, n_tile), lax.rem(here + n_tile - 2, n_tile)
    pair = here + 1 - 2 * lax.rem(here, 2)
    last = n_tile // 4
    grid_side = n_tile // 8 + 2
    side = 2 * n_chan * n_tile // grid_side

    def load(group):
        return pltpu.make_async_copy(
            volts.at[:, group], slab.at[group, pl.ds(0, FRAMES)], load_sem.at[group]
        )

    load_taps = pltpu.make_async_copy(taps_hbm, taps, taps_sem)
    load_taps.start()
    for group in range(GROUPS):
        load(group).start()

    barrier = pltpu.get_barrier_semaphore()

    def greet(step, _):
        peer = lax.rem(me + step, n_chan)
        pl.semaphore_signal(barrier, inc=1, device_id={"chan": peer}, device_id_type=MESH)
        return 0

    lax.fori_loop(1, n_chan, greet, 0)
    for other in (ahead, behind, pair):
        pl.semaphore_signal(barrier, inc=1, device_id={"tile": other}, device_id_type=MESH)

    fill_table(channels[...], table)
    load_taps.wait()

    for chunk in range(CHUNKS):

        def filter_step(group, _):
            if chunk == 0:
                load(group).wait()
            filter_group(group, chunk, slab, wide, taps, filtered)
            return 0

        lax.fori_loop(0, GROUPS, filter_step, 0)
        spectra = lax.dot_general(
            table[...], filtered[...], BY_LANES, preferred_element_type=jnp.float32
        )
        for part in (0, 1):
            for antenna in (0, 1):
                flag = flags[0, antenna].astype(jnp.float32)
                block = spectra[
                    part * n_chan : (part + 1) * n_chan, antenna * CHUNK : (antenna + 1) * CHUNK
                ]
                mixed[pl.ds(antenna, n_chan, stride=2), :] = block * flag
            packed = send[chunk].at[part].reshape(2 * n_chan, LANES)
            packed[...] = mixed[...].astype(packed.dtype)
        if chunk == 0:
            pl.semaphore_wait(barrier, n_chan - 1 + 3)

        def turn(step, _):
            peer = lax.rem(me + step, n_chan)
            pltpu.make_async_remote_copy(
                src_ref=send[chunk].at[:, peer], dst_ref=whole[chunk].at[:, here, me],
                send_sem=turn_send.at[chunk], recv_sem=turn_recv.at[chunk],
                device_id={"chan": peer}, device_id_type=MESH,
            ).start()
            return 0

        lax.fori_loop(1, n_chan, turn, 0)
        whole[chunk][:, here, me] = send[chunk][:, me]

    def turned(chunk):
        return pltpu.make_async_remote_copy(
            src_ref=send[chunk].at[:, pl.ds(0, n_chan - 1)],
            dst_ref=whole[chunk].at[:, here, pl.ds(0, n_chan - 1)],
            send_sem=turn_send.at[chunk], recv_sem=turn_recv.at[chunk],
            device_id={"chan": me}, device_id_type=MESH,
        )

    def across(chunk):
        block = whole[chunk].at[:, here]
        return pltpu.make_async_remote_copy(
            src_ref=block, dst_ref=block, send_sem=pair_send.at[chunk],
            recv_sem=pair_recv.at[chunk], device_id={"tile": pair}, device_id_type=MESH,
        )

    def hop(chunk, direction, column, step):
        base = here if column == 0 else pair
        back = -2 * (step - 1) if direction == 0 else 2 * (step - 1)
        block = lax.rem(base + n_tile + back, n_tile)
        piece = whole[chunk].at[direction, block] if step == last else whole[chunk].at[:, block]
        index = (chunk, direction, column, step - 1)
        return pltpu.make_async_remote_copy(
            src_ref=piece, dst_ref=piece, send_sem=ring_send.at[index],
            recv_sem=ring_recv.at[index],
            device_id={"tile": ahead if direction == 0 else behind}, device_id_type=MESH,
        )

    for chunk, column, step in RING_ORDER:
        if step == 1 and column == 0:
            turned(chunk).wait()
            across(chunk).start()
        if step == 1 and column == 1:
            across(chunk).wait_recv()
        for direction in (0, 1):
            if step > 1:
                hop(chunk, direction, column, step - 1).wait_recv()
            hop(chunk, direction, column, step).start()

    tile = tile_map[here, me]
    for chunk in range(CHUNKS):
        for column in (0, 1):
            for direction in (0, 1):
                hop(chunk, direction, column, last).wait_recv()
        across(chunk).wait_send()
        for _, column, step in [entry for entry in RING_ORDER if entry[0] == chunk]:
            for direction in (0, 1):
                hop(chunk, direction, column, step).wait_send()
        inputs = 2 * n_chan * n_tile
        flat = whole[chunk].reshape(2 * inputs, LANES)
        for part in (0, 1):
            for block in range(grid_side):
                gathered[block, :, part * LANES : (part + 1) * LANES] = flat[
                    pl.ds(part * inputs + block * side, side), :
                ]
        rows = gathered[lax.div(tile, grid_side)]
        straight = gathered[lax.rem(tile, grid_side)]
        crossed = jnp.concatenate([straight[:, LANES:], -straight[:, :LANES]], axis=1)
        for part, cols in enumerate((straight, crossed)):
            product = lax.dot_general(rows, cols, BY_LANES, preferred_element_type=jnp.float32)
            if chunk > 0:
                product = product + totals[part]
            if chunk < CHUNKS - 1:
                totals[part] = product
            else:
                out[0, 0, part] = (product * (1.0 / SPECTRA_SUMMED)).astype(out.dtype)


def on_device(voltages, fir_taps, channels, input_good_mask, tile_map):
    n_chan, n_tile = lax.axis_size("chan"), lax.axis_size("tile")
    side = 2 * n_chan * n_tile // (n_tile // 8 + 2)
    volts = voltages.reshape(2, FRAMES, GROUPS, LANES).transpose(1, 2, 0, 3)
    volts, fir_taps = (
        pltpu.with_memory_space_constraint(a, pltpu.HBM) for a in (volts, fir_taps)
    )
    vmem = pl.BlockSpec(memory_space=pltpu.VMEM)
    smem = pl.BlockSpec(memory_space=pltpu.SMEM)
    hbm = pl.BlockSpec(memory_space=pltpu.HBM)
    dma = pltpu.SemaphoreType.DMA
    hops = (CHUNKS, 2, 2, n_tile // 4)
    return pl.pallas_call(
        lambda *refs: kernel(n_chan, n_tile, *refs),
        name="channelize_correlate",
        out_shape=jax.ShapeDtypeStruct((1, 1, 2, side, side), jnp.bfloat16),
        in_specs=[hbm, hbm, vmem, smem, smem],
        out_specs=vmem,
        scratch_shapes=[
            pltpu.VMEM((GROUPS, FRAMES + 1, 2, LANES), jnp.bfloat16),
            pltpu.VMEM((FILTER_TAPS, TRANSFORM_LENGTH), jnp.float32),
            pltpu.VMEM((2 * (CHUNK + FILTER_TAPS), LANES), jnp.float32),
            pltpu.VMEM((2 * CHUNK, TRANSFORM_LENGTH), jnp.bfloat16),
            pltpu.VMEM((2 * n_chan, TRANSFORM_LENGTH), jnp.bfloat16),
            pltpu.VMEM((2 * n_chan, LANES), jnp.float32),
            pltpu.VMEM((n_tile // 8 + 2, side, 2 * LANES), jnp.bfloat16),
            pltpu.VMEM((2, side, side), jnp.float32),
            *[pltpu.VMEM((2, n_chan, 2, LANES), jnp.bfloat16)] * CHUNKS,
            *[pltpu.VMEM((2, n_tile, n_chan, 2, LANES), jnp.bfloat16)] * CHUNKS,
            dma((GROUPS,)),
            dma,
            dma((CHUNKS,)),
            dma((CHUNKS,)),
            dma(hops),
            dma(hops),
            dma((CHUNKS,)),
            dma((CHUNKS,)),
        ],
        compiler_params=pltpu.CompilerParams(
            collective_id=0, has_side_effects=True, vmem_limit_bytes=48 * 1024 * 1024
        ),
    )(volts, fir_taps, channels.reshape(1, -1), input_good_mask, tile_map.T)


def solution(mesh):
    in_specs = (P("tile", "chan", None), P(), P(), P("tile", "chan"), P())
    out_specs = P("chan", "tile", None, None, None)
    return jax.shard_map(
        on_device, mesh=mesh, in_specs=in_specs, out_specs=out_specs, check_vma=False
    )
```

```python
import math

import jax
import jax.numpy as jnp
from jax import lax
from jax.experimental import pallas as pl
from jax.experimental.pallas import tpu as pltpu
from jax.sharding import PartitionSpec as P

TRANSFORM_LENGTH = 2048
FILTER_TAPS = 16
SPECTRA_SUMMED = 256
MESH = pl.DeviceIdType.MESH

LANES = 128
GROUPS = TRANSFORM_LENGTH // LANES
FRAMES = SPECTRA_SUMMED + FILTER_TAPS - 1
CHUNK = LANES
CHUNKS = SPECTRA_SUMMED // CHUNK
BY_LANES = (((1,), (1,)), ((), ()))

RING_ORDER = (
    (0, 0, 1), (0, 0, 2), (0, 0, 3), (1, 0, 1), (0, 1, 1), (1, 0, 2), (0, 1, 2), (0, 0, 4),
    (1, 1, 1), (0, 1, 3), (1, 1, 2), (1, 0, 3), (1, 1, 3), (0, 1, 4), (1, 0, 4), (1, 1, 4),
)


def fill_table(channels_row, table):
    n = channels_row.shape[1]
    down = lax.broadcasted_iota(jnp.int32, (n, n), 0)
    along = lax.broadcasted_iota(jnp.int32, (n, n), 1)
    picked = jnp.where(down == along, channels_row.astype(jnp.float32), 0.0)
    lane = lax.broadcasted_iota(jnp.int32, (n, LANES), 1).astype(jnp.float32)
    phase = jnp.sum(picked, axis=1, keepdims=True) * lane
    low = phase - TRANSFORM_LENGTH * jnp.floor(phase * (1.0 / TRANSFORM_LENGTH))
    low = low * (2.0 * math.pi / TRANSFORM_LENGTH)
    high = phase - GROUPS * jnp.floor(phase * (1.0 / GROUPS))
    high = high * (2.0 * math.pi / GROUPS)
    factor = 1.0 / math.sqrt(TRANSFORM_LENGTH)
    cos_low, sin_low = jnp.cos(low) * factor, jnp.sin(low) * factor
    cos_high, sin_high = jnp.cos(high), jnp.sin(high)
    for group in range(GROUPS):
        lanes = pl.ds(group * LANES, LANES)
        cos_g, sin_g = cos_high[:, group : group + 1], sin_high[:, group : group + 1]
        table[pl.ds(0, n), lanes] = (cos_g * cos_low - sin_g * sin_low).astype(table.dtype)
        table[pl.ds(n, n), lanes] = (-(sin_g * cos_low + cos_g * sin_low)).astype(table.dtype)


def filter_group(group, chunk, slab, wide, taps, filtered):
    rows = 2 * (CHUNK + FILTER_TAPS)
    samples = slab.at[group].reshape(slab.shape[1] * 2, LANES)
    for row in range(0, rows, 16):
        wide[pl.ds(row, 16), :] = samples[pl.ds(2 * CHUNK * chunk + row, 16), :].astype(jnp.float32)
    lanes = pl.ds(group * LANES, LANES)
    weight = [jnp.broadcast_to(taps[pl.ds(j, 1), lanes], (8, LANES)) for j in range(FILTER_TAPS)]
    for antenna in (0, 1):
        for base in range(0, CHUNK, 64):
            total = [None] * 8
            for frame in range(64 + FILTER_TAPS - 8):
                window = wide[pl.ds(2 * (base + frame) + antenna, 8, stride=2), :]
                for part in range(8):
                    j = frame - 8 * part
                    if 0 <= j < FILTER_TAPS:
                        term = weight[j] * window
                        total[part] = term if total[part] is None else total[part] + term
            for part in range(0, 8, 2):
                pair = jnp.concatenate([total[part], total[part + 1]], axis=0)
                place = pl.ds(antenna * CHUNK + base + 8 * part, 16)
                filtered[place, lanes] = pair.astype(filtered.dtype)


def kernel(
    n_chan, n_tile, volts, taps_hbm, channels_hbm, flags_hbm, map_hbm, out,
    slab, taps, channels, flags, tile_map, wide, filtered, table, mixed, totals, *rest,
):
    send, whole = rest[:CHUNKS], rest[CHUNKS : 2 * CHUNKS]
    load_sem, small_sem, turn_send, turn_recv, ring_send, ring_recv, pair_send, pair_recv = rest[
        2 * CHUNKS :
    ]
    me = lax.axis_index("chan")
    here = lax.axis_index("tile")
    ahead, behind = lax.rem(here + 2, n_tile), lax.rem(here + n_tile - 2, n_tile)
    pair = here + 1 - 2 * lax.rem(here, 2)
    last = n_tile // 4
    grid_side = n_tile // 8 + 2
    side = 2 * n_chan * n_tile // grid_side

    def load(group):
        return pltpu.make_async_copy(
            volts.at[:, group], slab.at[group, pl.ds(0, FRAMES)], load_sem.at[group]
        )

    small = [
        pltpu.make_async_copy(source, target, small_sem.at[index])
        for index, (source, target) in enumerate(
            ((channels_hbm, channels), (taps_hbm, taps), (flags_hbm, flags), (map_hbm, tile_map))
        )
    ]
    for copy in small:
        copy.start()
    for group in range(GROUPS):
        load(group).start()

    barrier = pltpu.get_barrier_semaphore()

    def greet(step, _):
        peer = lax.rem(me + step, n_chan)
        pl.semaphore_signal(barrier, inc=1, device_id={"chan": peer}, device_id_type=MESH)
        return 0

    lax.fori_loop(1, n_chan, greet, 0)
    for other in (ahead, behind, pair):
        pl.semaphore_signal(barrier, inc=1, device_id={"tile": other}, device_id_type=MESH)

    small[0].wait()
    fill_table(channels[...], table)
    for copy in small[1:]:
        copy.wait()

    for chunk in range(CHUNKS):

        def filter_step(group, _):
            if chunk == 0:
                load(group).wait()
            filter_group(group, chunk, slab, wide, taps, filtered)
            return 0

        lax.fori_loop(0, GROUPS, filter_step, 0)
        spectra = lax.dot_general(
            table[...], filtered[...], BY_LANES, preferred_element_type=jnp.float32
        )
        for part in (0, 1):
            for antenna in (0, 1):
                flag = flags[0:1, antenna : antenna + 1].astype(jnp.float32)
                block = spectra[
                    part * n_chan : (part + 1) * n_chan, antenna * CHUNK : (antenna + 1) * CHUNK
                ]
                mixed[pl.ds(antenna, n_chan, stride=2), :] = block * flag
            packed = send[chunk].at[part].reshape(2 * n_chan, LANES)
            packed[...] = mixed[...].astype(packed.dtype)
        if chunk == 0:
            pl.semaphore_wait(barrier, n_chan - 1 + 3)

        def turn(step, _):
            peer = lax.rem(me + step, n_chan)
            pltpu.make_async_remote_copy(
                src_ref=send[chunk].at[:, peer], dst_ref=whole[chunk].at[:, here, me],
                send_sem=turn_send.at[chunk], recv_sem=turn_recv.at[chunk],
                device_id={"chan": peer}, device_id_type=MESH,
            ).start()
            return 0

        lax.fori_loop(1, n_chan, turn, 0)
        whole[chunk][:, here, me] = send[chunk][:, me]

    def turned(chunk):
        return pltpu.make_async_remote_copy(
            src_ref=send[chunk].at[:, pl.ds(0, n_chan - 1)],
            dst_ref=whole[chunk].at[:, here, pl.ds(0, n_chan - 1)],
            send_sem=turn_send.at[chunk], recv_sem=turn_recv.at[chunk],
            device_id={"chan": me}, device_id_type=MESH,
        )

    def across(chunk):
        block = whole[chunk].at[:, here]
        return pltpu.make_async_remote_copy(
            src_ref=block, dst_ref=block, send_sem=pair_send.at[chunk],
            recv_sem=pair_recv.at[chunk], device_id={"tile": pair}, device_id_type=MESH,
        )

    def hop(chunk, direction, column, step):
        base = here if column == 0 else pair
        back = -2 * (step - 1) if direction == 0 else 2 * (step - 1)
        block = lax.rem(base + n_tile + back, n_tile)
        piece = whole[chunk].at[direction, block] if step == last else whole[chunk].at[:, block]
        index = (chunk, direction, column, step - 1)
        return pltpu.make_async_remote_copy(
            src_ref=piece, dst_ref=piece, send_sem=ring_send.at[index],
            recv_sem=ring_recv.at[index],
            device_id={"tile": ahead if direction == 0 else behind}, device_id_type=MESH,
        )

    slot = tile_map[pl.ds(here, 1), :]
    mine = lax.broadcasted_iota(jnp.int32, slot.shape, 1) == me

    def weights(position):
        made = []
        for block in range(grid_side):
            hit = jnp.where(mine, jnp.where(position == block, 1.0, 0.0), 0.0)
            weight = jnp.sum(hit, axis=1, keepdims=True)
            weight = jnp.broadcast_to(weight, (16, LANES)).astype(jnp.bfloat16)
            made.append(jnp.concatenate([weight] * (side // 16), axis=0))
        return made

    row_weights = weights(lax.div(slot, grid_side))
    col_weights = weights(lax.rem(slot, grid_side))

    def chosen(flat, weight, part):
        picked = None
        for block in range(grid_side):
            term = flat[pl.ds((part * grid_side + block) * side, side), :] * weight[block]
            picked = term if picked is None else picked + term
        return picked

    for chunk, column, step in RING_ORDER:
        if step == 1 and column == 0:
            turned(chunk).wait()
            across(chunk).start()
        if step == 1 and column == 1:
            across(chunk).wait_recv()
        for direction in (0, 1):
            if step > 1:
                hop(chunk, direction, column, step - 1).wait_recv()
            hop(chunk, direction, column, step).start()

    for chunk in range(CHUNKS):
        for column in (0, 1):
            for direction in (0, 1):
                hop(chunk, direction, column, last).wait_recv()
        inputs = 2 * n_chan * n_tile
        flat = whole[chunk].reshape(2 * inputs, LANES)
        rows = jnp.concatenate([chosen(flat, row_weights, part) for part in (0, 1)], axis=1)
        col_real, col_imag = [chosen(flat, col_weights, part) for part in (0, 1)]
        straight = jnp.concatenate([col_real, col_imag], axis=1)
        crossed = jnp.concatenate([col_imag, -col_real], axis=1)
        for part, cols in enumerate((straight, crossed)):
            product = lax.dot_general(rows, cols, BY_LANES, preferred_element_type=jnp.float32)
            if chunk > 0:
                product = product + totals[part]
            if chunk < CHUNKS - 1:
                totals[part] = product
            else:
                out[0, 0, part] = (product * (1.0 / SPECTRA_SUMMED)).astype(out.dtype)
    for chunk in range(CHUNKS):
        across(chunk).wait_send()
    for chunk, column, step in RING_ORDER:
        for direction in (0, 1):
            hop(chunk, direction, column, step).wait_send()


def on_device(voltages, fir_taps, channels, input_good_mask, tile_map):
    n_chan, n_tile = lax.axis_size("chan"), lax.axis_size("tile")
    side = 2 * n_chan * n_tile // (n_tile // 8 + 2)
    volts = voltages.reshape(2, FRAMES, GROUPS, LANES).transpose(1, 2, 0, 3)
    operands = (volts, fir_taps, channels.reshape(1, -1), input_good_mask, tile_map.T)
    operands = [pltpu.with_memory_space_constraint(a, pltpu.HBM) for a in operands]
    vmem = pl.BlockSpec(memory_space=pltpu.VMEM)
    hbm = pl.BlockSpec(memory_space=pltpu.HBM)
    dma = pltpu.SemaphoreType.DMA
    hops = (CHUNKS, 2, 2, n_tile // 4)
    return pl.pallas_call(
        lambda *refs: kernel(n_chan, n_tile, *refs),
        name="channelize_correlate",
        out_shape=jax.ShapeDtypeStruct((1, 1, 2, side, side), jnp.bfloat16),
        in_specs=[hbm] * len(operands),
        out_specs=vmem,
        scratch_shapes=[
            pltpu.VMEM((GROUPS, FRAMES + 1, 2, LANES), jnp.bfloat16),
            *[pltpu.VMEM(a.shape, a.dtype) for a in operands[1:]],
            pltpu.VMEM((2 * (CHUNK + FILTER_TAPS), LANES), jnp.float32),
            pltpu.VMEM((2 * CHUNK, TRANSFORM_LENGTH), jnp.bfloat16),
            pltpu.VMEM((2 * n_chan, TRANSFORM_LENGTH), jnp.bfloat16),
            pltpu.VMEM((2 * n_chan, LANES), jnp.float32),
            pltpu.VMEM((2, side, side), jnp.float32),
            *[pltpu.VMEM((2, n_chan, 2, LANES), jnp.bfloat16)] * CHUNKS,
            *[pltpu.VMEM((2, n_tile, n_chan, 2, LANES), jnp.bfloat16)] * CHUNKS,
            dma((GROUPS,)),
            dma((4,)),
            dma((CHUNKS,)),
            dma((CHUNKS,)),
            dma(hops),
            dma(hops),
            dma((CHUNKS,)),
            dma((CHUNKS,)),
        ],
        compiler_params=pltpu.CompilerParams(
            collective_id=0, has_side_effects=True, vmem_limit_bytes=48 * 1024 * 1024
        ),
    )(*operands)


def solution(mesh):
    in_specs = (P("tile", "chan", None), P(), P(), P("tile", "chan"), P())
    out_specs = P("chan", "tile", None, None, None)
    return jax.shard_map(
        on_device, mesh=mesh, in_specs=in_specs, out_specs=out_specs, check_vma=False
    )
```

```python
import math

import jax
import jax.numpy as jnp
from jax import lax
from jax.experimental import pallas as pl
from jax.experimental.pallas import tpu as pltpu
from jax.sharding import PartitionSpec as P

TRANSFORM_LENGTH = 2048
FILTER_TAPS = 16
SPECTRA_SUMMED = 256
MESH = pl.DeviceIdType.MESH

LANES = 128
GROUPS = TRANSFORM_LENGTH // LANES
FRAMES = SPECTRA_SUMMED + FILTER_TAPS - 1
CHUNK = LANES
CHUNKS = SPECTRA_SUMMED // CHUNK
BY_LANES = (((1,), (1,)), ((), ()))

RING_ORDER = (
    (0, 0, 1), (0, 0, 2), (0, 0, 3), (1, 0, 1), (0, 1, 1), (1, 0, 2), (0, 1, 2), (0, 0, 4),
    (1, 1, 1), (0, 1, 3), (1, 1, 2), (1, 0, 3), (1, 1, 3), (0, 1, 4), (1, 0, 4), (1, 1, 4),
)


def fill_table(channels_row, table):
    n = channels_row.shape[1]
    down = lax.broadcasted_iota(jnp.int32, (n, n), 0)
    along = lax.broadcasted_iota(jnp.int32, (n, n), 1)
    picked = jnp.where(down == along, channels_row.astype(jnp.float32), 0.0)
    lane = lax.broadcasted_iota(jnp.int32, (n, LANES), 1).astype(jnp.float32)
    phase = jnp.sum(picked, axis=1, keepdims=True) * lane
    low = phase - TRANSFORM_LENGTH * jnp.floor(phase * (1.0 / TRANSFORM_LENGTH))
    low = low * (2.0 * math.pi / TRANSFORM_LENGTH)
    high = phase - GROUPS * jnp.floor(phase * (1.0 / GROUPS))
    high = high * (2.0 * math.pi / GROUPS)
    factor = 1.0 / math.sqrt(TRANSFORM_LENGTH)
    cos_low, sin_low = jnp.cos(low) * factor, jnp.sin(low) * factor
    cos_high, sin_high = jnp.cos(high), jnp.sin(high)
    for group in range(GROUPS):
        lanes = pl.ds(group * LANES, LANES)
        cos_g, sin_g = cos_high[:, group : group + 1], sin_high[:, group : group + 1]
        table[pl.ds(0, n), lanes] = (cos_g * cos_low - sin_g * sin_low).astype(table.dtype)
        table[pl.ds(n, n), lanes] = (-(sin_g * cos_low + cos_g * sin_low)).astype(table.dtype)


def filter_group(group, chunk, slab, wide, taps, filtered):
    rows = 2 * (CHUNK + FILTER_TAPS)
    samples = slab.at[group].reshape(slab.shape[1] * 2, LANES)
    for row in range(0, rows, 16):
        wide[pl.ds(row, 16), :] = samples[pl.ds(2 * CHUNK * chunk + row, 16), :].astype(jnp.float32)
    lanes = pl.ds(group * LANES, LANES)
    weight = [jnp.broadcast_to(taps[pl.ds(j, 1), lanes], (8, LANES)) for j in range(FILTER_TAPS)]
    for antenna in (0, 1):
        for base in range(0, CHUNK, 64):
            total = [None] * 8
            for frame in range(64 + FILTER_TAPS - 8):
                window = wide[pl.ds(2 * (base + frame) + antenna, 8, stride=2), :]
                for part in range(8):
                    j = frame - 8 * part
                    if 0 <= j < FILTER_TAPS:
                        term = weight[j] * window
                        total[part] = term if total[part] is None else total[part] + term
            for part in range(0, 8, 2):
                pair = jnp.concatenate([total[part], total[part + 1]], axis=0)
                place = pl.ds(antenna * CHUNK + base + 8 * part, 16)
                filtered[place, lanes] = pair.astype(filtered.dtype)


def kernel(
    n_chan, n_tile, volts, taps_hbm, channels_hbm, flags_hbm, map_hbm, out,
    slab, taps, channels, flags, tile_map, wide, filtered, table, mixed, totals, *rest,
):
    send, whole = rest[:CHUNKS], rest[CHUNKS : 2 * CHUNKS]
    load_sem, small_sem, turn_send, turn_recv, ring_send, ring_recv, pair_send, pair_recv = rest[
        2 * CHUNKS :
    ]
    me = lax.axis_index("chan")
    here = lax.axis_index("tile")
    ahead, behind = lax.rem(here + 2, n_tile), lax.rem(here + n_tile - 2, n_tile)
    pair = here + 1 - 2 * lax.rem(here, 2)
    last = n_tile // 4
    grid_side = n_tile // 8 + 2
    side = 2 * n_chan * n_tile // grid_side

    def load(group):
        return pltpu.make_async_copy(
            volts.at[:, group], slab.at[group, pl.ds(0, FRAMES)], load_sem.at[group]
        )

    small = [
        pltpu.make_async_copy(source, target, small_sem.at[index])
        for index, (source, target) in enumerate(
            ((channels_hbm, channels), (taps_hbm, taps), (flags_hbm, flags), (map_hbm, tile_map))
        )
    ]
    for copy in small:
        copy.start()
    for group in range(GROUPS):
        load(group).start()

    barrier = pltpu.get_barrier_semaphore()

    def greet(step, _):
        peer = lax.rem(me + step, n_chan)
        pl.semaphore_signal(barrier, inc=1, device_id={"chan": peer}, device_id_type=MESH)
        return 0

    lax.fori_loop(1, n_chan, greet, 0)
    for other in (ahead, behind, pair):
        pl.semaphore_signal(barrier, inc=1, device_id={"tile": other}, device_id_type=MESH)

    small[0].wait()
    fill_table(channels[...], table)
    for copy in small[1:]:
        copy.wait()

    for chunk in range(CHUNKS):

        def filter_step(group, _):
            if chunk == 0:
                load(group).wait()
            filter_group(group, chunk, slab, wide, taps, filtered)
            return 0

        lax.fori_loop(0, GROUPS, filter_step, 0)
        spectra = lax.dot_general(
            table[...], filtered[...], BY_LANES, preferred_element_type=jnp.float32
        )
        for part in (0, 1):
            for antenna in (0, 1):
                flag = flags[0:1, antenna : antenna + 1].astype(jnp.float32)
                block = spectra[
                    part * n_chan : (part + 1) * n_chan, antenna * CHUNK : (antenna + 1) * CHUNK
                ]
                mixed[pl.ds(antenna, n_chan, stride=2), :] = block * flag
            packed = send[chunk].at[part].reshape(2 * n_chan, LANES)
            packed[...] = mixed[...].astype(packed.dtype)
        if chunk == 0:
            pl.semaphore_wait(barrier, n_chan - 1 + 3)

        def turn(step, _):
            peer = lax.rem(me + step, n_chan)
            pltpu.make_async_remote_copy(
                src_ref=send[chunk].at[:, peer], dst_ref=whole[chunk].at[:, here, me],
                send_sem=turn_send.at[chunk], recv_sem=turn_recv.at[chunk],
                device_id={"chan": peer}, device_id_type=MESH,
            ).start()
            return 0

        lax.fori_loop(1, n_chan, turn, 0)
        whole[chunk][:, here, me] = send[chunk][:, me]

    def turned(chunk):
        return pltpu.make_async_remote_copy(
            src_ref=send[chunk].at[:, pl.ds(0, n_chan - 1)],
            dst_ref=whole[chunk].at[:, here, pl.ds(0, n_chan - 1)],
            send_sem=turn_send.at[chunk], recv_sem=turn_recv.at[chunk],
            device_id={"chan": me}, device_id_type=MESH,
        )

    def across(chunk):
        block = whole[chunk].at[:, here]
        return pltpu.make_async_remote_copy(
            src_ref=block, dst_ref=block, send_sem=pair_send.at[chunk],
            recv_sem=pair_recv.at[chunk], device_id={"tile": pair}, device_id_type=MESH,
        )

    def hop(chunk, direction, column, step):
        base = here if column == 0 else pair
        back = -2 * (step - 1) if direction == 0 else 2 * (step - 1)
        block = lax.rem(base + n_tile + back, n_tile)
        piece = whole[chunk].at[direction, block] if step == last else whole[chunk].at[:, block]
        index = (chunk, direction, column, step - 1)
        return pltpu.make_async_remote_copy(
            src_ref=piece, dst_ref=piece, send_sem=ring_send.at[index],
            recv_sem=ring_recv.at[index],
            device_id={"tile": ahead if direction == 0 else behind}, device_id_type=MESH,
        )

    slot = tile_map[pl.ds(here, 1), :]
    mine = lax.broadcasted_iota(jnp.int32, slot.shape, 1) == me

    def weights(position):
        made = []
        for block in range(grid_side):
            hit = jnp.where(mine, jnp.where(position == block, 1.0, 0.0), 0.0)
            weight = jnp.sum(hit, axis=1, keepdims=True)
            weight = jnp.broadcast_to(weight, (16, LANES)).astype(jnp.bfloat16)
            made.append(jnp.concatenate([weight] * (side // 16), axis=0))
        return made

    row_weights = weights(lax.div(slot, grid_side))
    col_weights = weights(lax.rem(slot, grid_side))

    def chosen(flat, weight, part):
        picked = None
        for block in range(grid_side):
            term = flat[pl.ds((part * grid_side + block) * side, side), :] * weight[block]
            picked = term if picked is None else picked + term
        return picked

    for chunk, column, step in RING_ORDER:
        if step == 1 and column == 0:
            turned(chunk).wait_recv()
            across(chunk).start()
        if step == 1 and column == 1:
            across(chunk).wait_recv()
        for direction in (0, 1):
            if step > 1:
                hop(chunk, direction, column, step - 1).wait_recv()
            hop(chunk, direction, column, step).start()

    for chunk in range(CHUNKS):
        for column in (0, 1):
            for direction in (0, 1):
                hop(chunk, direction, column, last).wait_recv()
        inputs = 2 * n_chan * n_tile
        flat = whole[chunk].reshape(2 * inputs, LANES)
        rows = jnp.concatenate([chosen(flat, row_weights, part) for part in (0, 1)], axis=1)
        col_real, col_imag = [chosen(flat, col_weights, part) for part in (0, 1)]
        straight = jnp.concatenate([col_real, col_imag], axis=1)
        crossed = jnp.concatenate([col_imag, -col_real], axis=1)
        for part, cols in enumerate((straight, crossed)):
            product = lax.dot_general(rows, cols, BY_LANES, preferred_element_type=jnp.float32)
            if chunk > 0:
                product = product + totals[part]
            if chunk < CHUNKS - 1:
                totals[part] = product
            else:
                out[0, 0, part] = (product * (1.0 / SPECTRA_SUMMED)).astype(out.dtype)
    for chunk in range(CHUNKS):
        turned(chunk).wait_send()
        across(chunk).wait_send()
    for chunk, column, step in RING_ORDER:
        for direction in (0, 1):
            hop(chunk, direction, column, step).wait_send()


def on_device(voltages, fir_taps, channels, input_good_mask, tile_map):
    n_chan, n_tile = lax.axis_size("chan"), lax.axis_size("tile")
    side = 2 * n_chan * n_tile // (n_tile // 8 + 2)
    volts = voltages.reshape(2, FRAMES, GROUPS, LANES).transpose(1, 2, 0, 3)
    operands = (volts, fir_taps, channels.reshape(1, -1), input_good_mask, tile_map.T)
    operands = [pltpu.with_memory_space_constraint(a, pltpu.HBM) for a in operands]
    vmem = pl.BlockSpec(memory_space=pltpu.VMEM)
    hbm = pl.BlockSpec(memory_space=pltpu.HBM)
    dma = pltpu.SemaphoreType.DMA
    hops = (CHUNKS, 2, 2, n_tile // 4)
    return pl.pallas_call(
        lambda *refs: kernel(n_chan, n_tile, *refs),
        name="channelize_correlate",
        out_shape=jax.ShapeDtypeStruct((1, 1, 2, side, side), jnp.bfloat16),
        in_specs=[hbm] * len(operands),
        out_specs=vmem,
        scratch_shapes=[
            pltpu.VMEM((GROUPS, FRAMES + 1, 2, LANES), jnp.bfloat16),
            *[pltpu.VMEM(a.shape, a.dtype) for a in operands[1:]],
            pltpu.VMEM((2 * (CHUNK + FILTER_TAPS), LANES), jnp.float32),
            pltpu.VMEM((2 * CHUNK, TRANSFORM_LENGTH), jnp.bfloat16),
            pltpu.VMEM((2 * n_chan, TRANSFORM_LENGTH), jnp.bfloat16),
            pltpu.VMEM((2 * n_chan, LANES), jnp.float32),
            pltpu.VMEM((2, side, side), jnp.float32),
            *[pltpu.VMEM((2, n_chan, 2, LANES), jnp.bfloat16)] * CHUNKS,
            *[pltpu.VMEM((2, n_tile, n_chan, 2, LANES), jnp.bfloat16)] * CHUNKS,
            dma((GROUPS,)),
            dma((4,)),
            dma((CHUNKS,)),
            dma((CHUNKS,)),
            dma(hops),
            dma(hops),
            dma((CHUNKS,)),
            dma((CHUNKS,)),
        ],
        compiler_params=pltpu.CompilerParams(
            collective_id=0, has_side_effects=True, vmem_limit_bytes=48 * 1024 * 1024
        ),
    )(*operands)


def solution(mesh):
    in_specs = (P("tile", "chan", None), P(), P(), P("tile", "chan"), P())
    out_specs = P("chan", "tile", None, None, None)
    return jax.shard_map(
        on_device, mesh=mesh, in_specs=in_specs, out_specs=out_specs, check_vma=False
    )
```
